32 devices in a mesh: dp: 16 (over z, y, core), mp: 2 (over x).
Axes of the slice: x: 2, y: 2, z: 4, core: 2. Of those that a mesh axis runs over, the one named last changes fastest.
Arguments:
- tokens: bfloat16 [2304, 4096], P('dp'), may hold values from -6 to 6
- cotangent: bfloat16 [2304, 4096], P('dp'), may hold values from -6 to 6
- gate_blocks: bfloat16 [16, 128, 128], P('dp'), may hold values from -0.5 to 0.5
- up_blocks: bfloat16 [16, 128, 128], P('dp'), may hold values from -0.5 to 0.5
- down_blocks: bfloat16 [16, 128, 128], P('dp'), may hold values from -0.5 to 0.5
- col_block: int32 [16], replicated, may hold values from 0 to 223, as said below
- in_row: int32 [16], replicated, may hold values from 0 to 31, as said below
- out_row: int32 [16], replicated, may hold values from 0 to 31
Outputs:
- input_grad: bfloat16 [2304, 4096], P('dp', 'mp')
- gate_grads: float32 [16, 128, 128], P('dp')
- up_grads: float32 [16, 128, 128], P('dp')
- down_grads: float32 [16, 128, 128], P('dp')
The draws below stay inside these ranges and needn't reach their ends.
Inputs may be any that keep to these rules, and one draw needn't show every extreme that they name: Flat blocks are ordered by owner: floor(col_block / 112) never falls along the list. Each owner holds 1 to 15 blocks, and some owner holds exactly 15. The pairs (in_row, col_block) are distinct, and so are the pairs (col_block, out_row). `in_row`: gate and up blocks share positions.
All inputs are finite; a program needn't handle non-finite values.
Results may differ from the reference program's by a relative error of at most 0.007.
Values may be sent and summed in bfloat16 or wider, within the bound.
No kernel may reach another device: no remote copies, remote signals or barrier semaphores. Data moves between devices by JAX's collectives and lax.ppermute only.
A program may use at most 64 MiB of HBM per device.

```python
import jax
import jax.numpy as jnp
from jax import lax

BLK = 128
D = 4096
FF = 28672
TOK_DEV = 144
NB = 16
CAP = 15
TOKENS = 2304
N_MP = 2


def pattern_draw(key):
    base_key = jax.random.fold_in(key, 4242)
    key_busy, key_weight, key_order, key_slots, key_shift = jax.random.split(base_key, 5)
    owners = jnp.arange(N_MP, dtype=jnp.int32)
    busy_owner = jax.random.randint(key_busy, (), 0, N_MP)
    weights = jnp.where(owners == busy_owner, 0, jax.random.randint(key_weight, (N_MP,), 1, 5))
    spare_units = NB - CAP - (N_MP - 1)
    shares = spare_units * weights // jnp.sum(weights)
    leftover = spare_units - jnp.sum(shares)
    owner_order = jax.random.permutation(key_order, N_MP)
    position = jnp.zeros((N_MP,), jnp.int32).at[owner_order].set(owners)
    busy_pos = position[busy_owner]
    ranked = position - (position > busy_pos).astype(jnp.int32)
    extra_unit = ((ranked < leftover) & (owners != busy_owner)).astype(jnp.int32)
    counts = jnp.where(owners == busy_owner, CAP, 1 + shares + extra_unit)
    starts = jnp.cumsum(counts) - counts
    flat_ids = jnp.arange(NB, dtype=jnp.int32)
    owner_ids = jnp.sum((flat_ids[:, None] >= starts[None, 1:]).astype(jnp.int32), axis=1)
    local_ids = flat_ids - starts[owner_ids]
    owned_cols = FF // (BLK * N_MP)
    row_blocks = D // BLK

    def owner_slots(owner_key):
        return jax.random.permutation(owner_key, row_blocks * owned_cols)
    slot_table = jax.vmap(owner_slots)(jax.random.split(key_slots, N_MP))
    chosen = slot_table[owner_ids, local_ids]
    col_local = chosen % owned_cols
    row_ids = chosen // owned_cols
    shifts = jax.random.randint(key_shift, (N_MP, owned_cols), 0, row_blocks)
    out_ids = (row_ids + shifts[owner_ids, col_local]) % row_blocks
    return ((owner_ids * owned_cols + col_local).astype(jnp.int32), row_ids.astype(jnp.int32), out_ids.astype(jnp.int32))


def draw_col_block(key, part):
    return pattern_draw(key)[0]


def draw_in_row(key, part):
    return pattern_draw(key)[1]


def draw_out_row(key, part):
    return pattern_draw(key)[2]


def steps_of(key, shape, pieces, least, top_value):
    def one(dim, parts):
        heights = jax.random.uniform(jax.random.fold_in(jax.random.fold_in(key, 6), dim), (parts,), jnp.float32, least / len(pieces), top_value / len(pieces))
        return jnp.repeat(jnp.exp(heights), shape[dim] // parts).reshape((-1,) + (1,) * (len(shape) - dim - 1))

    level = one(*pieces[0])
    for cut in pieces[1:]:
        level = level * one(*cut)
    return level


def noise(rng, shape, width, most, cuts=(), kind=jnp.bfloat16):
    array = jax.random.normal(rng, shape, jnp.float32) * width
    if len(cuts) > 0:
        array = steps_of(rng, shape, cuts, -0.22, 0.18) * array
    return jnp.clip(array, min=-most, max=most).astype(kind)


def setup_inputs(seed: int = 0) -> dict:
    keys = jax.random.split(jax.random.key(seed), 9)
    return {
        "tokens": noise(keys[0], (TOKENS, D), 1.0, 6.0, ((0, 16),)),
        "cotangent": noise(keys[1], (TOKENS, D), 1.0, 6.0, ((0, 16),)),
        "gate_blocks": noise(keys[2], (NB, BLK, BLK), BLK ** -0.5, 0.5, ((0, 16),)),
        "up_blocks": noise(keys[3], (NB, BLK, BLK), BLK ** -0.5, 0.5, ((0, 16),)),
        "down_blocks": noise(keys[4], (NB, BLK, BLK), BLK ** -0.5, 0.5, ((0, 16),)),
        "col_block": draw_col_block(jax.random.fold_in(keys[8], 71), 0),
        "in_row": draw_in_row(jax.random.fold_in(keys[8], 71), 0),
        "out_row": draw_out_row(jax.random.fold_in(keys[8], 71), 0),
    }


def reference(tokens, cotangent, gate_blocks, up_blocks, down_blocks, col_block, in_row, out_row):
    highest = lax.Precision.HIGHEST
    row_blocks = D // BLK
    owned_cols = FF // (BLK * N_MP)
    owner_of = col_block // owned_cols
    same_column = (col_block[:, None] == col_block[None, :]).astype(jnp.float32)
    owner_onehot = (owner_of[None, :] == jnp.arange(N_MP, dtype=jnp.int32)[:, None]).astype(jnp.float32)
    row_onehot = (in_row[:, None] == jnp.arange(row_blocks, dtype=jnp.int32)[None, :]).astype(jnp.float32)
    gate_full = gate_blocks.astype(jnp.float32)
    up_full = up_blocks.astype(jnp.float32)
    down_full = down_blocks.astype(jnp.float32)
    groups = TOKENS // TOK_DEV
    token_groups = tokens.reshape(groups, TOK_DEV, row_blocks, BLK)
    cot_groups = cotangent.reshape(groups, TOK_DEV, row_blocks, BLK)

    def one_group(totals, tiles):
        token_tile, cot_tile = tiles
        token_in = jnp.take(token_tile, in_row, axis=1).astype(jnp.float32)
        cot_in = jnp.take(cot_tile, out_row, axis=1).astype(jnp.float32)
        gate_part = jnp.einsum('tkb,kbc->ktc', token_in, gate_full, precision=highest)
        up_part = jnp.einsum('tkb,kbc->ktc', token_in, up_full, precision=highest)
        gate_total = jnp.einsum('jk,ktc->jtc', same_column, gate_part, precision=highest)
        up_total = jnp.einsum('jk,ktc->jtc', same_column, up_part, precision=highest)
        gate_sigmoid = jax.nn.sigmoid(gate_total)
        gate_act = gate_total * gate_sigmoid
        hidden = (gate_act * up_total).astype(jnp.bfloat16)
        down_part = jnp.einsum('tkb,kcb->ktc', cot_in, down_full, precision=highest)
        hidden_grad = jnp.einsum('jk,ktc->jtc', same_column, down_part, precision=highest)
        gate_grad = (hidden_grad * up_total * gate_sigmoid * (1.0 + gate_total * (1.0 - gate_sigmoid))).astype(jnp.bfloat16)
        up_grad = (hidden_grad * gate_act).astype(jnp.bfloat16)
        down_term = jnp.einsum('ktc,tkb->kcb', hidden.astype(jnp.float32), cot_in, precision=highest)
        gate_term = jnp.einsum('tkb,ktc->kbc', token_in, gate_grad.astype(jnp.float32), precision=highest)
        up_term = jnp.einsum('tkb,ktc->kbc', token_in, up_grad.astype(jnp.float32), precision=highest)
        spread = jnp.einsum('ktc,kbc->ktb', gate_grad.astype(jnp.float32), gate_full, precision=highest)
        spread = spread + jnp.einsum('ktc,kbc->ktb', up_grad.astype(jnp.float32), up_full, precision=highest)
        owner_parts = jnp.einsum('mk,kr,ktb->mtrb', owner_onehot, row_onehot, spread, precision=highest)
        rounded = lax.optimization_barrier(owner_parts.astype(jnp.bfloat16)).astype(jnp.float32)
        input_tile = jnp.sum(rounded, axis=0).astype(jnp.bfloat16).reshape(TOK_DEV, D)
        return (totals[0] + gate_term, totals[1] + up_term, totals[2] + down_term), input_tile

    zeros_grad = jnp.zeros((NB, BLK, BLK), jnp.float32)
    totals, input_tiles = lax.scan(one_group, (zeros_grad, zeros_grad, zeros_grad), (token_groups, cot_groups))
    grad_scale = TOKENS ** -0.5
    return (input_tiles.reshape(TOKENS, D), totals[0] * grad_scale, totals[1] * grad_scale, totals[2] * grad_scale)
```

```python
import functools

import jax
import jax.numpy as jnp
from jax import lax
from jax.experimental import pallas as pl
from jax.experimental.pallas import tpu as pltpu
from jax.sharding import PartitionSpec as P

VMEM = pltpu.MemorySpace.VMEM
SMEM = pltpu.MemorySpace.SMEM
F32 = jnp.float32
BF16 = jnp.bfloat16


def dot(a, b, dim_a, dim_b):
    return lax.dot_general(a, b, (((dim_a,), (dim_b,)), ((), ())), preferred_element_type=F32)


def repeat(count, body):
    if count <= 16:
        for i in range(count):
            body(i)
    else:

        def step(i, carry):
            body(i)
            return carry

        lax.fori_loop(0, count, step, 0)


def pack_kernel(rank_ref, gate_ref, up_ref, down_ref, out_ref, turned):
    share = out_ref.shape[1] // 3
    first = pl.multiple_of(rank_ref[0] * share, share)
    for i in range(gate_ref.shape[0]):
        turned[...] = gate_ref[i].astype(F32).T
        out_ref[i, :share] = turned[pl.ds(first, share), :].astype(BF16)
        turned[...] = up_ref[i].astype(F32).T
        out_ref[i, share : 2 * share] = turned[pl.ds(first, share), :].astype(BF16)
        turned[...] = down_ref[i].astype(F32)
        out_ref[i, 2 * share :] = turned[pl.ds(first, share), :].astype(BF16)


def layer_kernel(rank_ref, col_ref, in_ref, out_row_ref, tok_ref, cot_ref, w_ref, *rest, ranks):
    spread_refs, (grad_ref, gu, dh, gu_grad, hidden, total) = rest[:ranks], rest[ranks:]
    count, rows, block = w_ref.shape
    share = rows // 3
    two = 2 * share
    rank = rank_ref[0]

    def columns(ref, index):
        return ref[:, pl.ds(pl.multiple_of(index * block, block), block)]

    def leader(k):
        return lax.fori_loop(
            0, k, lambda j, best: jnp.where(col_ref[k - 1 - j] == col_ref[k], k - 1 - j, best), k
        )

    def forward(k):
        gu[k] = dot(w_ref[k, :two], columns(tok_ref, in_ref[k]), 1, 1)
        dh[k] = dot(w_ref[k, two:], columns(cot_ref, out_row_ref[k]), 1, 1)

    repeat(count, forward)
    total[...] = jnp.zeros_like(total)
    heads = [leader(k) for k in range(count)] if count <= 16 else None

    def head(k):
        return heads[k] if heads is not None else leader(k)

    def join(k):
        first = head(k)

        @pl.when(first != k)
        def _():
            gu[first] += gu[k]
            dh[first] += dh[k]

    repeat(count, join)

    def middle(k):
        gate, up, grad = gu[k, :share], gu[k, share:], dh[k]
        sig = jax.nn.sigmoid(gate)
        act = gate * sig
        hidden[k] = (act * up).astype(BF16)
        gu_grad[k, :share] = (grad * up * sig * (1.0 + gate * (1.0 - sig))).astype(BF16)
        gu_grad[k, share:] = (grad * act).astype(BF16)

    repeat(count, middle)

    def spread(k):
        total[in_ref[k]] += dot(gu_grad[head(k)], w_ref[k, :two], 0, 0)

    repeat(count, spread)
    for d in range(ranks):
        per = total.shape[0] // ranks
        for r in range(per):
            spread_refs[d][:, r * block : (r + 1) * block] = total[(rank ^ d) * per + r].astype(BF16)

    def backward(k):
        first = head(k)
        grad_ref[k, :two] = dot(gu_grad[first], columns(tok_ref, in_ref[k]), 1, 0).astype(BF16)
        grad_ref[k, two:] = dot(hidden[first], columns(cot_ref, out_row_ref[k]), 1, 0).astype(BF16)

    repeat(count, backward)


def sum_kernel(parts_ref, out_ref, *, scale):
    total = parts_ref[0].astype(F32)
    for i in range(1, parts_ref.shape[0]):
        total += parts_ref[i].astype(F32)
    out_ref[...] = total * scale


def place_kernel(rank_ref, *refs, ranks):
    pieces, (gate_ref, up_ref, down_ref, whole) = refs[:ranks], refs[ranks:]
    share = pieces[0].shape[1] // 3
    for i in range(gate_ref.shape[0]):
        for part, ref in enumerate((gate_ref, up_ref, down_ref)):
            for d in range(ranks):
                at = pl.multiple_of((rank_ref[0] ^ d) * share, share)
                whole[pl.ds(at, share), :] = pieces[d][i, part * share : (part + 1) * share]
            ref[i] = whole[...] if part == 2 else whole[...].T


def call(kernel, out_shape, scalars, arrays, scratch=()):
    return pl.pallas_call(
        kernel,
        out_shape=out_shape,
        in_specs=[pl.BlockSpec(memory_space=SMEM)] * scalars + [pl.BlockSpec(memory_space=VMEM)] * arrays,
        out_specs=jax.tree.map(lambda _: pl.BlockSpec(memory_space=VMEM), out_shape),
        scratch_shapes=list(scratch),
    )


def on_device(tokens, cotangent, gate_blocks, up_blocks, down_blocks, col_block, in_row, out_row):
    shape = jax.ShapeDtypeStruct
    token_count, width = tokens.shape
    local, block, _ = gate_blocks.shape
    count = col_block.shape[0]
    groups, ranks = lax.axis_size("dp"), lax.axis_size("mp")
    share = block // ranks
    rank = lax.axis_index("mp").astype(jnp.int32).reshape(1)
    scale = (token_count * groups) ** -0.5

    own = call(
        pack_kernel, shape((local, 3 * share, block), BF16), 1, 3, [pltpu.VMEM((block, block), F32)]
    )(rank, gate_blocks, up_blocks, down_blocks)
    weights = lax.all_gather(own, "dp", axis=0, tiled=True)
    *spread, grads = call(
        functools.partial(layer_kernel, ranks=ranks),
        [shape((token_count, width // ranks), BF16)] * ranks + [shape((count, 3 * share, block), BF16)],
        4,
        3,
        [
            pltpu.VMEM((count, 2 * share, token_count), F32),
            pltpu.VMEM((count, share, token_count), F32),
            pltpu.VMEM((count, 2 * share, token_count), BF16),
            pltpu.VMEM((count, share, token_count), BF16),
            pltpu.VMEM((width // block, token_count, block), F32),
        ],
    )(rank, col_block, in_row, out_row, tokens, cotangent, weights)

    def across(x, d):
        return lax.ppermute(x, "mp", [(i, i ^ d) for i in range(ranks)])

    arrived = [across(spread[d], d) for d in range(1, ranks)]
    parts = lax.all_to_all(
        grads.reshape(groups, local * 3 * share, block), "dp", 0, 0, tiled=True
    ).reshape(groups, local, 3 * share, block)
    summed = call(functools.partial(sum_kernel, scale=scale), shape((local, 3 * share, block), F32), 0, 1)(parts)
    pieces = [summed] + [across(summed, d) for d in range(1, ranks)]
    grad_shape = shape((local, block, block), F32)
    gate_grads, up_grads, down_grads = call(
        functools.partial(place_kernel, ranks=ranks),
        [grad_shape] * 3,
        1,
        ranks,
        [pltpu.VMEM((block, block), F32)],
    )(rank, *pieces)
    input_grad = spread[0].astype(F32)
    for piece in arrived:
        input_grad = input_grad + piece.astype(F32)
    return input_grad.astype(BF16), gate_grads, up_grads, down_grads


def solution(mesh):
    flat = P("dp", None, None)
    return jax.shard_map(
        on_device,
        mesh=mesh,
        in_specs=(P("dp", None), P("dp", None), flat, flat, flat, P(), P(), P()),
        out_specs=(P("dp", "mp"), flat, flat, flat),
        check_vma=False,
    )
```

```python
import functools

import jax
import jax.numpy as jnp
from jax import lax
from jax.experimental import pallas as pl
from jax.experimental.pallas import tpu as pltpu
from jax.sharding import PartitionSpec as P

VMEM = pltpu.MemorySpace.VMEM
SMEM = pltpu.MemorySpace.SMEM
F32 = jnp.float32
BF16 = jnp.bfloat16


def dot(a, b, dim_a, dim_b):
    return lax.dot_general(a, b, (((dim_a,), (dim_b,)), ((), ())), preferred_element_type=F32)


def pack_kernel(rank_ref, gate_ref, up_ref, down_ref, out_ref, turned):
    share = out_ref.shape[1] // 3
    first = pl.multiple_of(rank_ref[0] * share, share)
    for i in range(gate_ref.shape[0]):
        turned[...] = gate_ref[i].astype(F32).T
        out_ref[i, :share] = turned[pl.ds(first, share), :].astype(BF16)
        turned[...] = up_ref[i].astype(F32).T
        out_ref[i, share : 2 * share] = turned[pl.ds(first, share), :].astype(BF16)
        turned[...] = down_ref[i].astype(F32)
        out_ref[i, 2 * share :] = turned[pl.ds(first, share), :].astype(BF16)


def layer_kernel(place_ref, col_ref, in_ref, out_row_ref, tok_ref, cot_ref, near_ref, far_ref, *rest, ranks, local):
    spread_refs, (near_grad, far_grad, gu, dh, gu_grad, hidden, total) = rest[:ranks], rest[ranks:]
    half, rows, block = near_ref.shape
    count = 2 * half
    share = rows // 3
    two = 2 * share
    me, rank = place_ref[0], place_ref[1]
    quarter = half // local // 2

    def flat(slot):
        at, inner = slot // local, slot % local
        side, pair, far = at // (2 * quarter), (at // quarter) % 2, at % quarter
        return (me ^ (far * 4 + pair * 2 + side)) * local + inner

    def weight(slot, first, last):
        return (near_ref if slot < half else far_ref)[slot % half, first:last]

    def columns(ref, index):
        return ref[:, pl.ds(pl.multiple_of(index * block, block), block)]

    keys = [flat(slot) for slot in range(count)]
    cols = [col_ref[key] for key in keys]
    rows_in = [in_ref[key] for key in keys]
    rows_out = [out_row_ref[key] for key in keys]
    heads = []
    for slot in range(count):
        best = jnp.int32(slot)
        for earlier in reversed(range(slot)):
            best = jnp.where(cols[earlier] == cols[slot], earlier, best)
        heads.append(best)

    for slot in range(count):
        gu[slot] = dot(weight(slot, 0, two), columns(tok_ref, rows_in[slot]), 1, 1)
        dh[slot] = dot(weight(slot, two, rows), columns(cot_ref, rows_out[slot]), 1, 1)
    total[...] = jnp.zeros_like(total)
    for slot in range(1, count):

        @pl.when(heads[slot] != slot)
        def _(slot=slot):
            gu[heads[slot]] += gu[slot]
            dh[heads[slot]] += dh[slot]

    for slot in range(count):
        gate, up, grad = gu[slot, :share], gu[slot, share:], dh[slot]
        sig = jax.nn.sigmoid(gate)
        act = gate * sig
        hidden[slot] = (act * up).astype(BF16)
        gu_grad[slot, :share] = (grad * up * sig * (1.0 + gate * (1.0 - sig))).astype(BF16)
        gu_grad[slot, share:] = (grad * act).astype(BF16)
    for slot in range(count):
        total[rows_in[slot]] += dot(gu_grad[heads[slot]], weight(slot, 0, two), 0, 0)
    per = total.shape[0] // ranks
    for d in range(ranks):
        for r in range(per):
            spread_refs[d][:, r * block : (r + 1) * block] = total[(rank ^ d) * per + r].astype(BF16)
    for slot in range(count):
        ref, at = (near_grad if slot < half else far_grad), slot % half
        ref[at, :two] = dot(gu_grad[heads[slot]], columns(tok_ref, rows_in[slot]), 1, 0).astype(BF16)
        ref[at, two:] = dot(hidden[heads[slot]], columns(cot_ref, rows_out[slot]), 1, 0).astype(BF16)


def place_kernel(rank_ref, *refs, ranks):
    pieces, (gate_ref, up_ref, down_ref, whole) = refs[:ranks], refs[ranks:]
    share = pieces[0].shape[1] // 3
    for i in range(gate_ref.shape[0]):
        for part, ref in enumerate((gate_ref, up_ref, down_ref)):
            for d in range(ranks):
                at = pl.multiple_of((rank_ref[0] ^ d) * share, share)
                whole[pl.ds(at, share), :] = pieces[d][i, part * share : (part + 1) * share]
            ref[i] = whole[...] if part == 2 else whole[...].T


def call(kernel, out_shape, scalars, arrays, scratch=()):
    return pl.pallas_call(
        kernel,
        out_shape=out_shape,
        in_specs=[pl.BlockSpec(memory_space=SMEM)] * scalars + [pl.BlockSpec(memory_space=VMEM)] * arrays,
        out_specs=jax.tree.map(lambda _: pl.BlockSpec(memory_space=VMEM), out_shape),
        scratch_shapes=list(scratch),
    )


def on_device(tokens, cotangent, gate_blocks, up_blocks, down_blocks, col_block, in_row, out_row):
    shape = jax.ShapeDtypeStruct
    token_count, width = tokens.shape
    local, block, _ = gate_blocks.shape
    count = col_block.shape[0]
    groups, ranks = lax.axis_size("dp"), lax.axis_size("mp")
    share = block // ranks
    rank = lax.axis_index("mp").astype(jnp.int32).reshape(1)
    scale = (token_count * groups) ** -0.5

    def along(x, axis, size, d):
        return lax.ppermute(x, axis, [(i, i ^ d) for i in range(size)])

    def over(x, d):
        return along(x, "dp", groups, d)

    own = call(
        pack_kernel, shape((local, 3 * share, block), BF16), 1, 3, [pltpu.VMEM((block, block), F32)]
    )(rank, gate_blocks, up_blocks, down_blocks)
    fars = groups // 4
    quarter = fars * local
    column = jnp.concatenate([own] + [over(own, 4 * i) for i in range(1, fars)], axis=0)
    near = jnp.concatenate([column, over(column, 2)], axis=0)
    far = over(near, 1)
    place = jnp.concatenate([lax.axis_index("dp").astype(jnp.int32).reshape(1), rank])
    grad_parts = shape((2 * quarter, 3 * share, block), BF16)
    *spread, near_grad, far_grad = call(
        functools.partial(layer_kernel, ranks=ranks, local=local),
        [shape((token_count, width // ranks), BF16)] * ranks + [grad_parts] * 2,
        4,
        4,
        [
            pltpu.VMEM((count, 2 * share, token_count), F32),
            pltpu.VMEM((count, share, token_count), F32),
            pltpu.VMEM((count, 2 * share, token_count), BF16),
            pltpu.VMEM((count, share, token_count), BF16),
            pltpu.VMEM((width // block, token_count, block), F32),
        ],
    )(place, col_block, in_row, out_row, tokens, cotangent, near, far)

    def across(x, d):
        return along(x, "mp", ranks, d)

    arrived = [across(spread[d], d) for d in range(1, ranks)]
    chip = near_grad.astype(F32) + over(far_grad, 1).astype(F32)
    plane = chip[:quarter] + over(chip[quarter:].astype(BF16), 2).astype(F32)
    summed = plane[:local]
    for i in range(1, fars):
        piece = plane[i * local : (i + 1) * local].astype(BF16)
        summed = summed + over(piece, 4 * i).astype(F32)
    summed = summed * scale
    pieces = [summed] + [across(summed, d) for d in range(1, ranks)]
    grad_shape = shape((local, block, block), F32)
    gate_grads, up_grads, down_grads = call(
        functools.partial(place_kernel, ranks=ranks),
        [grad_shape] * 3,
        1,
        ranks,
        [pltpu.VMEM((block, block), F32)],
    )(rank, *pieces)
    input_grad = spread[0].astype(F32)
    for piece in arrived:
        input_grad = input_grad + piece.astype(F32)
    return input_grad.astype(BF16), gate_grads, up_grads, down_grads


def solution(mesh):
    flat = P("dp", None, None)
    return jax.shard_map(
        on_device,
        mesh=mesh,
        in_specs=(P("dp", None), P("dp", None), flat, flat, flat, P(), P(), P()),
        out_specs=(P("dp", "mp"), flat, flat, flat),
        check_vma=False,
    )
```

```python
import functools

import jax
import jax.numpy as jnp
from jax import lax
from jax.experimental import pallas as pl
from jax.experimental.pallas import tpu as pltpu
from jax.sharding import PartitionSpec as P

VMEM = pltpu.MemorySpace.VMEM
SMEM = pltpu.MemorySpace.SMEM
HBM = pltpu.MemorySpace.HBM
F32 = jnp.float32
BF16 = jnp.bfloat16


def dot(a, b, dim_a, dim_b):
    return lax.dot_general(a, b, (((dim_a,), (dim_b,)), ((), ())), preferred_element_type=F32)


def pack_kernel(rank_ref, gate_ref, up_ref, down_ref, out_ref, held, turned, sems):
    share = out_ref.shape[1] // 3
    first = pl.multiple_of(rank_ref[0] * share, share)
    copies = [
        pltpu.make_async_copy(ref, held.at[part], sems.at[part])
        for part, ref in enumerate((gate_ref, up_ref, down_ref))
    ]
    for copy in copies:
        copy.start()
    for part, copy in enumerate(copies):
        copy.wait()
        for i in range(out_ref.shape[0]):
            whole = held[part, i].astype(F32)
            turned[...] = whole if part == 2 else whole.T
            out_ref[i, part * share : (part + 1) * share] = turned[pl.ds(first, share), :].astype(BF16)


class Slots:
    def __init__(self, me, count, local):
        self.count, self.half, self.quarter = count, count // 2, count // 4
        self.keys = []
        for slot in range(count):
            at, inner = slot // local, slot % local
            fars = self.quarter // local
            side, pair, far = at // (2 * fars), (at // fars) % 2, at % fars
            self.keys.append((me ^ (far * 4 + pair * 2 + side)) * local + inner)

    def heads(self, col_ref):
        cols = [col_ref[key] for key in self.keys]
        found = []
        for slot in range(self.count):
            best = jnp.int32(slot)
            for earlier in reversed(range(slot)):
                best = jnp.where(cols[earlier] == cols[slot], earlier, best)
            found.append(best)
        return found


def forward(w_ref, at, tok, cot, gu_ref, dh_ref, to):
    two = gu_ref.shape[1]
    gu_ref[to] = dot(w_ref[at, :two], tok, 1, 1)
    dh_ref[to] = dot(w_ref[at, two:], cot, 1, 1)


def backward(grad_ref, at, gu_grad, hidden, tok, cot):
    two = gu_grad.shape[0]
    grad_ref[at, :two] = dot(gu_grad, tok, 1, 0).astype(BF16)
    grad_ref[at, two:] = dot(hidden, cot, 1, 0).astype(BF16)


def first_kernel(me_ref, in_ref, out_row_ref, tokens, cotangent, w_ref, tok_ref, cot_ref, gu_ref, dh_ref, sems, *, local):
    count, _, block = tok_ref.shape
    slots = Slots(me_ref[0], count, local)

    def column(array, index):
        return array.at[:, pl.ds(pl.multiple_of(index * block, block), block)]

    copies = []
    for slot, key in enumerate(slots.keys):
        copies.append(
            (
                pltpu.make_async_copy(column(tokens, in_ref[key]), tok_ref.at[slot], sems.at[0, slot]),
                pltpu.make_async_copy(column(cotangent, out_row_ref[key]), cot_ref.at[slot], sems.at[1, slot]),
            )
        )
        for copy in copies[-1]:
            copy.start()
    for pair in copies:
        for copy in pair:
            copy.wait()
    for slot in range(slots.quarter):
        forward(w_ref, slot, tok_ref[slot], cot_ref[slot], gu_ref, dh_ref, slot)


def second_kernel(w_ref, tok_ref, cot_ref, gu_ref, dh_ref):
    quarter = w_ref.shape[0]
    for slot in range(quarter):
        forward(w_ref, slot, tok_ref[quarter + slot], cot_ref[quarter + slot], gu_ref, dh_ref, slot)


def third_kernel(
    me_ref, col_ref, w_ref, tok_ref, cot_ref, gu0, gu1, dh0, dh1, grad_ref, gu_grad, hidden, gu, dh, *, local
):
    count, two, _ = gu_grad.shape
    share = two // 2
    slots = Slots(me_ref[0], count, local)
    heads = slots.heads(col_ref)
    half, quarter = slots.half, slots.quarter
    for slot in range(quarter):
        gu[slot], gu[quarter + slot] = gu0[slot], gu1[slot]
        dh[slot], dh[quarter + slot] = dh0[slot], dh1[slot]
    for slot in range(half, count):
        forward(w_ref, slot - half, tok_ref[slot], cot_ref[slot], gu, dh, slot)
    for slot in range(1, count):

        @pl.when(heads[slot] != slot)
        def _(slot=slot):
            gu[heads[slot]] += gu[slot]
            dh[heads[slot]] += dh[slot]

    for slot in range(count):
        gate, up, grad = gu[slot, :share], gu[slot, share:], dh[slot]
        sig = jax.nn.sigmoid(gate)
        act = gate * sig
        hidden[slot] = (act * up).astype(BF16)
        gu_grad[slot, :share] = (grad * up * sig * (1.0 + gate * (1.0 - sig))).astype(BF16)
        gu_grad[slot, share:] = (grad * act).astype(BF16)
    for slot in range(half, count):
        head = heads[slot]
        backward(grad_ref, slot - half, gu_grad[head], hidden[head], tok_ref[slot], cot_ref[slot])


def fourth_kernel(
    me_ref, rank_ref, col_ref, in_ref, near_ref, far_ref, tok_ref, cot_ref, gu_grad, hidden, *rest, ranks, local
):
    spread_refs, (grad_ref, total) = rest[:ranks], rest[ranks:]
    count, two, _ = gu_grad.shape
    block = tok_ref.shape[2]
    slots = Slots(me_ref[0], count, local)
    heads = slots.heads(col_ref)
    half = slots.half
    total[...] = jnp.zeros_like(total)
    for slot in range(count):
        weight = near_ref[slot, :two] if slot < half else far_ref[slot - half, :two]
        total[in_ref[slots.keys[slot]]] += dot(gu_grad[heads[slot]], weight, 0, 0)
    per = total.shape[0] // ranks
    for d in range(ranks):
        for r in range(per):
            spread_refs[d][:, r * block : (r + 1) * block] = total[(rank_ref[0] ^ d) * per + r].astype(BF16)
    for slot in range(half):
        head = heads[slot]
        backward(grad_ref, slot, gu_grad[head], hidden[head], tok_ref[slot], cot_ref[slot])


def place_kernel(rank_ref, *refs, ranks):
    pieces, (gate_ref, up_ref, down_ref, whole) = refs[:ranks], refs[ranks:]
    share = pieces[0].shape[1] // 3
    for i in range(gate_ref.shape[0]):
        for part, ref in enumerate((gate_ref, up_ref, down_ref)):
            for d in range(ranks):
                at = pl.multiple_of((rank_ref[0] ^ d) * share, share)
                whole[pl.ds(at, share), :] = pieces[d][i, part * share : (part + 1) * share].astype(F32)
            ref[i] = whole[...] if part == 2 else whole[...].T


def call(kernel, out_shape, spaces, scratch=(), mib=4, flops=0):
    where = {"s": SMEM, "h": HBM, "v": VMEM}
    return pl.pallas_call(
        kernel,
        out_shape=out_shape,
        in_specs=[pl.BlockSpec(memory_space=where[c]) for c in spaces],
        out_specs=jax.tree.map(lambda _: pl.BlockSpec(memory_space=VMEM), out_shape),
        scratch_shapes=list(scratch),
        compiler_params=pltpu.CompilerParams(vmem_limit_bytes=mib << 20),
        cost_estimate=pl.CostEstimate(flops=flops, bytes_accessed=flops // 256, transcendentals=0) if flops else None,
    )


def outside(x):
    return pltpu.with_memory_space_constraint(x, HBM)


def on_device(tokens, cotangent, gate_blocks, up_blocks, down_blocks, col_block, in_row, out_row):
    token_count, width = tokens.shape
    local, block, _ = gate_blocks.shape
    count = col_block.shape[0]
    groups, ranks = lax.axis_size("dp"), lax.axis_size("mp")
    share = block // ranks
    two, rows = 2 * share, 3 * share
    fars = groups // 4
    quarter = fars * local
    me = lax.axis_index("dp").astype(jnp.int32).reshape(1)
    rank = lax.axis_index("mp").astype(jnp.int32).reshape(1)
    scale = (token_count * groups) ** -0.5
    macs = 2 * token_count * block * rows

    def f32(*dims):
        return jax.ShapeDtypeStruct(dims, F32)

    def bf16(*dims):
        return jax.ShapeDtypeStruct(dims, BF16)

    def along(x, axis, size, d):
        return lax.ppermute(x, axis, [(i, i ^ d) for i in range(size)])

    def over(x, d):
        return along(x, "dp", groups, d)

    def across(x, d):
        return along(x, "mp", ranks, d)

    own = call(
        pack_kernel,
        bf16(local, rows, block),
        "shhh",
        [
            pltpu.VMEM((3, local, block, block), BF16),
            pltpu.VMEM((block, block), F32),
            pltpu.SemaphoreType.DMA((3,)),
        ],
    )(rank, *map(outside, (gate_blocks, up_blocks, down_blocks)))
    column = jnp.concatenate([own] + [over(own, 4 * i) for i in range(1, fars)], axis=0)
    beside = over(column, 2)
    some_gu, some_dh = f32(quarter, two, token_count), f32(quarter, share, token_count)
    tok, cot, gu0, dh0 = call(
        functools.partial(first_kernel, local=local),
        [bf16(count, token_count, block)] * 2 + [some_gu, some_dh],
        "ssshhv",
        [pltpu.SemaphoreType.DMA((2, count))],
        8,
        macs * quarter,
    )(me, in_row, out_row, outside(tokens), outside(cotangent), column)
    beside, tok = lax.optimization_barrier((beside, tok))
    near = jnp.concatenate([column, beside], axis=0)
    far = over(near, 1)
    gu1, dh1 = call(second_kernel, [some_gu, some_dh], "vvv", (), 8, macs * quarter)(beside, tok, cot)
    grad_parts = bf16(2 * quarter, rows, block)
    far_grad, gu_grad, hidden = call(
        functools.partial(third_kernel, local=local),
        [grad_parts, bf16(count, two, token_count), bf16(count, share, token_count)],
        "ssvvvvvvv",
        [pltpu.VMEM((count, two, token_count), F32), pltpu.VMEM((count, share, token_count), F32)],
        12,
        macs * count,
    )(me, col_block, far, tok, cot, gu0, gu1, dh0, dh1)
    *spread, near_grad = call(
        functools.partial(fourth_kernel, ranks=ranks, local=local),
        [bf16(token_count, width // ranks)] * ranks + [grad_parts],
        "ssssvvvvvv",
        [pltpu.VMEM((width // block, token_count, block), F32)],
        12,
        macs * count,
    )(me, rank, col_block, in_row, near, far, tok, cot, gu_grad, hidden)

    arrived = [across(spread[d], d) for d in range(1, ranks)]
    chip = near_grad.astype(F32) + over(far_grad, 1).astype(F32)
    plane = chip[:quarter] + over(chip[quarter:].astype(BF16), 2).astype(F32)
    summed = plane[:local]
    for i in range(1, fars):
        piece = plane[i * local : (i + 1) * local].astype(BF16)
        summed = summed + over(piece, 4 * i).astype(F32)
    summed = summed * scale
    pieces = [summed] + [across(summed.astype(BF16), d) for d in range(1, ranks)]
    gate_grads, up_grads, down_grads = call(
        functools.partial(place_kernel, ranks=ranks),
        [f32(local, block, block)] * 3,
        "s" + "v" * ranks,
        [pltpu.VMEM((block, block), F32)],
    )(rank, *pieces)
    input_grad = spread[0].astype(F32)
    for piece in arrived:
        input_grad = input_grad + piece.astype(F32)
    return input_grad.astype(BF16), gate_grads, up_grads, down_grads


def solution(mesh):
    flat = P("dp", None, None)
    return jax.shard_map(
        on_device,
        mesh=mesh,
        in_specs=(P("dp", None), P("dp", None), flat, flat, flat, P(), P(), P()),
        out_specs=(P("dp", "mp"), flat, flat, flat),
        check_vma=False,
    )
```

```python
import functools

import jax
import jax.numpy as jnp
from jax import lax
from jax.experimental import pallas as pl
from jax.experimental.pallas import tpu as pltpu
from jax.sharding import PartitionSpec as P


VMEM = pltpu.MemorySpace.VMEM
SMEM = pltpu.MemorySpace.SMEM
HBM = pltpu.MemorySpace.HBM
F32 = jnp.float32
BF16 = jnp.bfloat16


def dot(a, b, dim_a, dim_b):
    return lax.dot_general(a, b, (((dim_a,), (dim_b,)), ((), ())), preferred_element_type=F32)


def pack_kernel(rank_ref, gate_ref, up_ref, down_ref, out_ref, held, turned, sems):
    share = out_ref.shape[1] // 3
    first = pl.multiple_of(rank_ref[0] * share, share)
    copies = [
        pltpu.make_async_copy(ref, held.at[part], sems.at[part])
        for part, ref in enumerate((gate_ref, up_ref, down_ref))
    ]
    for copy in copies:
        copy.start()
    for part, copy in enumerate(copies):
        copy.wait()
        for i in range(out_ref.shape[0]):
            whole = held[part, i].astype(F32)
            turned[...] = whole if part == 2 else whole.T
            out_ref[i, part * share : (part + 1) * share] = turned[pl.ds(first, share), :].astype(BF16)


class Slots:
    def __init__(self, me, count, local):
        self.count, self.half, self.quarter = count, count // 2, count // 4
        self.keys = []
        for slot in range(count):
            at, inner = slot // local, slot % local
            fars = self.quarter // local
            side, pair, far = at // (2 * fars), (at // fars) % 2, at % fars
            self.keys.append((me ^ (far * 4 + pair * 2 + side)) * local + inner)

    def heads(self, col_ref):
        cols = [col_ref[key] for key in self.keys]
        found = []
        for slot in range(self.count):
            best = jnp.int32(slot)
            for earlier in reversed(range(slot)):
                best = jnp.where(cols[earlier] == cols[slot], earlier, best)
            found.append(best)
        return found


def forward(w_ref, at, tok, cot, gu_ref, dh_ref, to):
    two = gu_ref.shape[1]
    gu_ref[to] = dot(w_ref[at, :two], tok, 1, 1)
    dh_ref[to] = dot(w_ref[at, two:], cot, 1, 1)


def backward(grad_ref, at, gu_grad, hidden, tok, cot):
    two = gu_grad.shape[0]
    grad_ref[at, :two] = dot(gu_grad, tok, 1, 0).astype(BF16)
    grad_ref[at, two:] = dot(hidden, cot, 1, 0).astype(BF16)


def collect_kernel(me_ref, index_ref, array, out_ref, sems, *, local):
    count, _, block = out_ref.shape
    copies = []
    for slot, key in enumerate(Slots(me_ref[0], count, local).keys):
        at = pl.ds(pl.multiple_of(index_ref[key] * block, block), block)
        copies.append(pltpu.make_async_copy(array.at[:, at], out_ref.at[slot], sems.at[slot]))
    for copy in copies:
        copy.start()
    for copy in copies:
        copy.wait()


def forward_kernel(w_ref, tok_ref, cot_ref, gu_ref, dh_ref, *, first):
    for slot in range(w_ref.shape[0]):
        forward(w_ref, slot, tok_ref[first + slot], cot_ref[first + slot], gu_ref, dh_ref, slot)


def third_kernel(
    me_ref, col_ref, w_ref, tok_ref, cot_ref, gu0, gu1, dh0, dh1, grad_ref, gu_grad, hidden, gu, dh, *, local
):
    count, two, _ = gu_grad.shape
    share = two // 2
    slots = Slots(me_ref[0], count, local)
    heads = slots.heads(col_ref)
    half, quarter = slots.half, slots.quarter
    for slot in range(quarter):
        gu[slot], gu[quarter + slot] = gu0[slot], gu1[slot]
        dh[slot], dh[quarter + slot] = dh0[slot], dh1[slot]
    for slot in range(half, count):
        forward(w_ref, slot - half, tok_ref[slot], cot_ref[slot], gu, dh, slot)
    for slot in range(1, count):

        @pl.when(heads[slot] != slot)
        def _(slot=slot):
            gu[heads[slot]] += gu[slot]
            dh[heads[slot]] += dh[slot]

    for slot in range(count):
        gate, up, grad = gu[slot, :share], gu[slot, share:], dh[slot]
        sig = jax.nn.sigmoid(gate)
        act = gate * sig
        hidden[slot] = (act * up).astype(BF16)
        gu_grad[slot, :share] = (grad * up * sig * (1.0 + gate * (1.0 - sig))).astype(BF16)
        gu_grad[slot, share:] = (grad * act).astype(BF16)
    for slot in range(half, count):
        head = heads[slot]
        backward(grad_ref, slot - half, gu_grad[head], hidden[head], tok_ref[slot], cot_ref[slot])


def fourth_kernel(
    me_ref, rank_ref, col_ref, in_ref, near_ref, far_ref, tok_ref, cot_ref, gu_grad, hidden, *rest, ranks, local
):
    spread_refs, (grad_ref, total) = rest[:ranks], rest[ranks:]
    count, two, _ = gu_grad.shape
    block = tok_ref.shape[2]
    slots = Slots(me_ref[0], count, local)
    heads = slots.heads(col_ref)
    half = slots.half
    total[...] = jnp.zeros_like(total)
    for slot in range(count):
        weight = near_ref[slot, :two] if slot < half else far_ref[slot - half, :two]
        total[in_ref[slots.keys[slot]]] += dot(gu_grad[heads[slot]], weight, 0, 0)
    per = total.shape[0] // ranks
    for d in range(ranks):
        for r in range(per):
            spread_refs[d][:, r * block : (r + 1) * block] = total[(rank_ref[0] ^ d) * per + r].astype(BF16)
    for slot in range(half):
        head = heads[slot]
        backward(grad_ref, slot, gu_grad[head], hidden[head], tok_ref[slot], cot_ref[slot])


def place_kernel(rank_ref, *refs, ranks):
    pieces, (gate_ref, up_ref, down_ref, whole) = refs[:ranks], refs[ranks:]
    share = pieces[0].shape[1] // 3
    for i in range(gate_ref.shape[0]):
        for part, ref in enumerate((gate_ref, up_ref, down_ref)):
            for d in range(ranks):
                at = pl.multiple_of((rank_ref[0] ^ d) * share, share)
                whole[pl.ds(at, share), :] = pieces[d][i, part * share : (part + 1) * share].astype(F32)
            ref[i] = whole[...] if part == 2 else whole[...].T


def call(kernel, out_shape, spaces, scratch=(), mib=4, flops=0):
    where = {"s": SMEM, "h": HBM, "v": VMEM}
    return pl.pallas_call(
        kernel,
        out_shape=out_shape,
        in_specs=[pl.BlockSpec(memory_space=where[c]) for c in spaces],
        out_specs=jax.tree.map(lambda _: pl.BlockSpec(memory_space=VMEM), out_shape),
        scratch_shapes=list(scratch),
        compiler_params=pltpu.CompilerParams(vmem_limit_bytes=mib << 20),
        cost_estimate=pl.CostEstimate(flops=flops, bytes_accessed=flops // 256, transcendentals=0) if flops else None,
    )


def outside(x):
    return pltpu.with_memory_space_constraint(x, HBM)


def on_device(tokens, cotangent, gate_blocks, up_blocks, down_blocks, col_block, in_row, out_row):
    token_count, width = tokens.shape
    local, block, _ = gate_blocks.shape
    count = col_block.shape[0]
    groups, ranks = lax.axis_size("dp"), lax.axis_size("mp")
    share = block // ranks
    two, rows = 2 * share, 3 * share
    fars = groups // 4
    quarter = fars * local
    me = lax.axis_index("dp").astype(jnp.int32).reshape(1)
    rank = lax.axis_index("mp").astype(jnp.int32).reshape(1)
    scale = (token_count * groups) ** -0.5
    macs = 2 * token_count * block * rows

    def f32(*dims):
        return jax.ShapeDtypeStruct(dims, F32)

    def bf16(*dims):
        return jax.ShapeDtypeStruct(dims, BF16)

    def along(x, axis, size, d):
        return lax.ppermute(x, axis, [(i, i ^ d) for i in range(size)])

    def over(x, d):
        return along(x, "dp", groups, d)

    def across(x, d):
        return along(x, "mp", ranks, d)

    own = call(
        pack_kernel,
        bf16(local, rows, block),
        "shhh",
        [
            pltpu.VMEM((3, local, block, block), BF16),
            pltpu.VMEM((block, block), F32),
            pltpu.SemaphoreType.DMA((3,)),
        ],
    )(rank, *map(outside, (gate_blocks, up_blocks, down_blocks)))
    across_z = [over(own, 4 * i) for i in range(1, fars)]
    beside_own, beside_next = over(own, 2), over(own, 6)
    column = jnp.concatenate([own] + across_z, axis=0)
    onward = over(jnp.concatenate(across_z[1:], axis=0), 2)
    beside = jnp.concatenate([beside_own, beside_next, onward], axis=0)

    def collect(array, index):
        return call(
            functools.partial(collect_kernel, local=local),
            bf16(count, token_count, block),
            "ssh",
            [pltpu.SemaphoreType.DMA((count,))],
            4,
            macs * quarter,
        )(me, outside(index), outside(array))

    tok = collect(tokens, in_row)
    cot = collect(cotangent, out_row)

    def some_forward(weights, index):
        kernel = functools.partial(forward_kernel, first=index * quarter)
        out = [f32(quarter, two, token_count), f32(quarter, share, token_count)]
        return call(kernel, out, "vvv", (), 8, macs * quarter)(weights, tok, cot)

    gu0, dh0 = some_forward(column, 0)
    beside, gu0 = lax.optimization_barrier((beside, gu0))
    near = jnp.concatenate([column, beside], axis=0)
    far = over(near, 1)
    gu1, dh1 = some_forward(beside, 1)
    grad_parts = bf16(2 * quarter, rows, block)
    far_grad, gu_grad, hidden = call(
        functools.partial(third_kernel, local=local),
        [grad_parts, bf16(count, two, token_count), bf16(count, share, token_count)],
        "ssvvvvvvv",
        [pltpu.VMEM((count, two, token_count), F32), pltpu.VMEM((count, share, token_count), F32)],
        12,
        macs * count,
    )(me, col_block, far, tok, cot, gu0, gu1, dh0, dh1)
    *spread, near_grad = call(
        functools.partial(fourth_kernel, ranks=ranks, local=local),
        [bf16(token_count, width // ranks)] * ranks + [grad_parts],
        "ssssvvvvvv",
        [pltpu.VMEM((width // block, token_count, block), F32)],
        12,
        macs * count,
    )(me, rank, col_block, in_row, near, far, tok, cot, gu_grad, hidden)

    arrived = [across(spread[d], d) for d in range(1, ranks)]
    chip = near_grad.astype(F32) + over(far_grad, 1).astype(F32)
    onward = over(chip[quarter + 2 * local :].astype(BF16), 2).astype(F32)
    summed = chip[:local]
    for i in range(2, fars):
        piece = chip[i * local : (i + 1) * local] + onward[(i - 2) * local : (i - 1) * local]
        summed = summed + over(piece.astype(BF16), 4 * i).astype(F32)
    for first, d in ((local, 4), (quarter, 2), (quarter + local, 6)):
        summed = summed + over(chip[first : first + local].astype(BF16), d).astype(F32)
    summed = summed * scale
    pieces = [summed] + [across(summed.astype(BF16), d) for d in range(1, ranks)]
    input_grad = spread[0].astype(F32)
    for piece in arrived:
        input_grad = input_grad + piece.astype(F32)
    input_grad, *pieces = lax.optimization_barrier((input_grad.astype(BF16), *pieces))
    gate_grads, up_grads, down_grads = call(
        functools.partial(place_kernel, ranks=ranks),
        [f32(local, block, block)] * 3,
        "s" + "v" * ranks,
        [pltpu.VMEM((block, block), F32)],
    )(rank, *pieces)
    return input_grad, gate_grads, up_grads, down_grads


def solution(mesh):
    flat = P("dp", None, None)
    return jax.shard_map(
        on_device,
        mesh=mesh,
        in_specs=(P("dp", None), P("dp", None), flat, flat, flat, P(), P(), P()),
        out_specs=(P("dp", "mp"), flat, flat, flat),
        check_vma=False,
    )
```

```python
import functools

import jax
import jax.numpy as jnp
from jax import lax
from jax.experimental import pallas as pl
from jax.experimental.pallas import tpu as pltpu
from jax.sharding import PartitionSpec as P


VMEM = pltpu.MemorySpace.VMEM
SMEM = pltpu.MemorySpace.SMEM
HBM = pltpu.MemorySpace.HBM
F32 = jnp.float32
BF16 = jnp.bfloat16


def dot(a, b, dim_a, dim_b):
    return lax.dot_general(a, b, (((dim_a,), (dim_b,)), ((), ())), preferred_element_type=F32)


def pack_kernel(gate_ref, up_ref, down_ref, out_ref, held, turned, sems):
    share = out_ref.shape[1] // 3
    first = pl.multiple_of(lax.axis_index("mp") * share, share)
    copies = [
        pltpu.make_async_copy(ref, held.at[part], sems.at[part])
        for part, ref in enumerate((gate_ref, up_ref, down_ref))
    ]
    for copy in copies:
        copy.start()
    for part, copy in enumerate(copies):
        copy.wait()
        for i in range(out_ref.shape[0]):
            whole = held[part, i].astype(F32)
            turned[...] = whole if part == 2 else whole.T
            out_ref[i, part * share : (part + 1) * share] = turned[pl.ds(first, share), :].astype(BF16)


class Slots:
    def __init__(self, count, local):
        me = lax.axis_index("dp")
        self.count, self.half, self.quarter = count, count // 2, count // 4
        self.keys = []
        for slot in range(count):
            at, inner = slot // local, slot % local
            fars = self.quarter // local
            side, pair, far = at // (2 * fars), (at // fars) % 2, at % fars
            self.keys.append((me ^ (far * 4 + pair * 2 + side)) * local + inner)

    def heads(self, col_ref, count):
        cols = [col_ref[key] for key in self.keys[:count]]
        found = []
        for slot in range(count):
            best = jnp.int32(slot)
            for earlier in reversed(range(slot)):
                best = jnp.where(cols[earlier] == cols[slot], earlier, best)
            found.append(best)
        return found


def forward(w_ref, at, tok, cot, gu_ref, dh_ref, to):
    two = gu_ref.shape[1]
    gu_ref[to] = dot(w_ref[at, :two], tok, 1, 1)
    dh_ref[to] = dot(w_ref[at, two:], cot, 1, 1)


def backward(grad_ref, at, gu_grad, hidden, tok, cot):
    two = gu_grad.shape[0]
    grad_ref[at, :two] = dot(gu_grad, tok, 1, 0).astype(BF16)
    grad_ref[at, two:] = dot(hidden, cot, 1, 0).astype(BF16)


def bring_kernel(array, out_ref, sem):
    copy = pltpu.make_async_copy(array, out_ref, sem)
    copy.start()
    copy.wait()


def collect_kernel(in_ref, out_row_ref, tokens, cotangent, tok_ref, cot_ref, sems, *, local):
    count, _, block = cot_ref.shape
    slots = Slots(count, local)
    copies = []
    for slot, key in enumerate(slots.keys):
        at = pl.ds(pl.multiple_of(out_row_ref[key] * block, block), block)
        copies.append(pltpu.make_async_copy(cotangent.at[:, at], cot_ref.at[slot], sems.at[slot]))
    for copy in copies:
        copy.start()
    for slot, key in enumerate(slots.keys):
        tok_ref[slot] = tokens[:, pl.ds(pl.multiple_of(in_ref[key] * block, block), block)]
    for copy in copies:
        copy.wait()


def middle(slot, gu, dh, gu_grad, hidden):
    share = dh.shape[1]
    gate, up, grad = gu[slot, :share], gu[slot, share:], dh[slot]
    sig = jax.nn.sigmoid(gate)
    act = gate * sig
    hidden[slot] = (act * up).astype(BF16)
    gu_grad[slot, :share] = (grad * up * sig * (1.0 + gate * (1.0 - sig))).astype(BF16)
    gu_grad[slot, share:] = (grad * act).astype(BF16)


def join(slot, head, gu, dh):
    @pl.when(head != slot)
    def _():
        gu[head] += gu[slot]
        dh[head] += dh[slot]


def first_kernel(w_ref, tok_ref, cot_ref, gu, dh):
    for slot in range(w_ref.shape[0]):
        forward(w_ref, slot, tok_ref[slot], cot_ref[slot], gu, dh, slot)


def second_kernel(cols, w_ref, tok_ref, cot_ref, gu_in, dh_in, gu, dh, gu_grad, hidden, col_ref, sem, *, local):
    del gu_in, dh_in
    copy = pltpu.make_async_copy(cols, col_ref, sem)
    copy.start()
    slots = Slots(gu.shape[0], local)
    for slot in range(slots.quarter, slots.half):
        forward(w_ref, slot - slots.quarter, tok_ref[slot], cot_ref[slot], gu, dh, slot)
    copy.wait()
    heads = slots.heads(col_ref, slots.half)
    for slot in range(1, slots.half):
        join(slot, heads[slot], gu, dh)
    for slot in range(slots.half):
        middle(slot, gu, dh, gu_grad, hidden)


def third_kernel(
    cols,
    w_ref,
    tok_ref,
    cot_ref,
    gu_in,
    dh_in,
    gg_in,
    hid_in,
    grad_ref,
    gu,
    dh,
    gu_grad,
    hidden,
    col_ref,
    sem,
    *,
    local,
):
    del gu_in, dh_in, gg_in, hid_in
    slots = Slots(gu.shape[0], local)
    count, half = slots.count, slots.half
    copy = pltpu.make_async_copy(cols, col_ref, sem)
    copy.start()
    for slot in range(half, count):
        forward(w_ref, slot - half, tok_ref[slot], cot_ref[slot], gu, dh, slot)
    copy.wait()
    heads = slots.heads(col_ref, count)
    shared = jnp.bool_(False)
    for slot in range(half, count):
        shared = shared | (heads[slot] != slot)

    @pl.when(shared)
    def _():
        for slot in range(half, count):
            join(slot, heads[slot], gu, dh)
        for near in range(half):
            changed = heads[half] == near
            for slot in range(half + 1, count):
                changed = changed | (heads[slot] == near)

            @pl.when(changed)
            def _(near=near):
                middle(near, gu, dh, gu_grad, hidden)

    for slot in range(half, count):
        middle(slot, gu, dh, gu_grad, hidden)
    for slot in range(half, count):
        head = heads[slot]
        backward(grad_ref, slot - half, gu_grad[head], hidden[head], tok_ref[slot], cot_ref[slot])


def fourth_kernel(cols, rows_in, near_ref, far_ref, tok_ref, cot_ref, gu_grad, hidden, *rest, ranks, local):
    spread_refs, (grad_ref, total, col_ref, in_ref, sems) = rest[:ranks], rest[ranks:]
    count, two, _ = gu_grad.shape
    block = tok_ref.shape[2]
    copies = [
        pltpu.make_async_copy(cols, col_ref, sems.at[0]),
        pltpu.make_async_copy(rows_in, in_ref, sems.at[1]),
    ]
    for copy in copies:
        copy.start()
    slots = Slots(count, local)
    half = slots.half
    rank = lax.axis_index("mp")
    total[...] = jnp.zeros_like(total)
    for copy in copies:
        copy.wait()
    heads = slots.heads(col_ref, count)
    for slot in range(count):
        weight = near_ref[slot, :two] if slot < half else far_ref[slot - half, :two]
        total[in_ref[slots.keys[slot]]] += dot(gu_grad[heads[slot]], weight, 0, 0)
    per = total.shape[0] // ranks
    for d in range(ranks):
        for r in range(per):
            spread_refs[d][:, r * block : (r + 1) * block] = total[(rank ^ d) * per + r].astype(BF16)
    for slot in range(half):
        head = heads[slot]
        backward(grad_ref, slot, gu_grad[head], hidden[head], tok_ref[slot], cot_ref[slot])


def place_kernel(*refs, ranks):
    pieces, (gate_ref, up_ref, down_ref, whole) = refs[:ranks], refs[ranks:]
    share = pieces[0].shape[1] // 3
    for i in range(gate_ref.shape[0]):
        for part, ref in enumerate((gate_ref, up_ref, down_ref)):
            for d in range(ranks):
                at = pl.multiple_of((lax.axis_index("mp") ^ d) * share, share)
                whole[pl.ds(at, share), :] = pieces[d][i, part * share : (part + 1) * share].astype(F32)
            ref[i] = whole[...] if part == 2 else whole[...].T


def call(kernel, out_shape, spaces, scratch=(), mib=4, flops=0, aliases=None):
    where = {"s": SMEM, "h": HBM, "v": VMEM}
    return pl.pallas_call(
        kernel,
        out_shape=out_shape,
        in_specs=[pl.BlockSpec(memory_space=where[c]) for c in spaces],
        out_specs=jax.tree.map(lambda _: pl.BlockSpec(memory_space=VMEM), out_shape),
        scratch_shapes=list(scratch),
        input_output_aliases=aliases or {},
        compiler_params=pltpu.CompilerParams(vmem_limit_bytes=mib << 20),
        cost_estimate=pl.CostEstimate(flops=flops, bytes_accessed=flops // 256, transcendentals=0) if flops else None,
    )


def outside(x):
    return pltpu.with_memory_space_constraint(x, HBM)


def on_device(tokens, cotangent, gate_blocks, up_blocks, down_blocks, col_block, in_row, out_row):
    token_count, width = tokens.shape
    local, block, _ = gate_blocks.shape
    count = col_block.shape[0]
    groups, ranks = lax.axis_size("dp"), lax.axis_size("mp")
    share = block // ranks
    two, rows = 2 * share, 3 * share
    fars = groups // 4
    quarter = fars * local
    scale = (token_count * groups) ** -0.5
    macs = 2 * token_count * block * rows

    def f32(*dims):
        return jax.ShapeDtypeStruct(dims, F32)

    def bf16(*dims):
        return jax.ShapeDtypeStruct(dims, BF16)

    def along(x, axis, size, d):
        return lax.ppermute(x, axis, [(i, i ^ d) for i in range(size)])

    def over(x, d):
        return along(x, "dp", groups, d)

    def across(x, d):
        return along(x, "mp", ranks, d)

    own = call(
        pack_kernel,
        bf16(local, rows, block),
        "hhh",
        [
            pltpu.VMEM((3, local, block, block), BF16),
            pltpu.VMEM((block, block), F32),
            pltpu.SemaphoreType.DMA((3,)),
        ],
    )(*map(outside, (gate_blocks, up_blocks, down_blocks)))
    across_z = [over(own, 4 * i) for i in range(1, fars)]
    beside_own, beside_next = over(own, 2), over(own, 6)
    column = jnp.concatenate([own] + across_z, axis=0)
    onward = over(jnp.concatenate(across_z[1:], axis=0), 2)
    beside = jnp.concatenate([beside_own, beside_next, onward], axis=0)
    held = call(
        bring_kernel, bf16(token_count, width), "h", [pltpu.SemaphoreType.DMA], 4, macs * quarter
    )(outside(tokens))
    tok, cot = call(
        functools.partial(collect_kernel, local=local),
        [bf16(count, token_count, block)] * 2,
        "ssvh",
        [pltpu.SemaphoreType.DMA((count,))],
        6,
        macs * quarter,
    )(outside(in_row), outside(out_row), held, outside(cotangent))
    cols = outside(col_block)
    sums = [f32(count, two, token_count), f32(count, share, token_count)]
    grads = [bf16(count, two, token_count), bf16(count, share, token_count)]
    gu, dh = call(first_kernel, sums, "vvv", (), 12, macs * quarter)(column, tok, cot)
    beside, gu = lax.optimization_barrier((beside, gu))
    near = jnp.concatenate([column, beside], axis=0)
    far = over(near, 1)
    gu, dh, gu_grad, hidden = call(
        functools.partial(second_kernel, local=local),
        sums + grads,
        "hvvvvv",
        [pltpu.SMEM((count,), jnp.int32), pltpu.SemaphoreType.DMA],
        12,
        macs * quarter,
        {4: 0, 5: 1},
    )(cols, beside, tok, cot, gu, dh)
    grad_parts = bf16(2 * quarter, rows, block)
    far_grad, _, _, gu_grad, hidden = call(
        functools.partial(third_kernel, local=local),
        [grad_parts] + sums + grads,
        "hvvvvvvv",
        [pltpu.SMEM((count,), jnp.int32), pltpu.SemaphoreType.DMA],
        12,
        macs * count,
        {4: 1, 5: 2, 6: 3, 7: 4},
    )(cols, far, tok, cot, gu, dh, gu_grad, hidden)
    *spread, near_grad = call(
        functools.partial(fourth_kernel, ranks=ranks, local=local),
        [bf16(token_count, width // ranks)] * ranks + [grad_parts],
        "hhvvvvvv",
        [
            pltpu.VMEM((width // block, token_count, block), F32),
            pltpu.SMEM((count,), jnp.int32),
            pltpu.SMEM((count,), jnp.int32),
            pltpu.SemaphoreType.DMA((2,)),
        ],
        12,
        macs * count,
    )(cols, outside(in_row), near, far, tok, cot, gu_grad, hidden)

    arrived = [across(spread[d], d) for d in range(1, ranks)]
    chip = near_grad.astype(F32) + over(far_grad, 1).astype(F32)
    onward = over(chip[quarter + 2 * local :].astype(BF16), 2).astype(F32)
    summed = chip[:local]
    for i in range(2, fars):
        piece = chip[i * local : (i + 1) * local] + onward[(i - 2) * local : (i - 1) * local]
        summed = summed + over(piece.astype(BF16), 4 * i).astype(F32)
    for first, d in ((local, 4), (quarter, 2), (quarter + local, 6)):
        summed = summed + over(chip[first : first + local].astype(BF16), d).astype(F32)
    summed = summed * scale
    pieces = [summed] + [across(summed.astype(BF16), d) for d in range(1, ranks)]
    input_grad = spread[0].astype(F32)
    for piece in arrived:
        input_grad = input_grad + piece.astype(F32)
    input_grad, *pieces = lax.optimization_barrier((input_grad.astype(BF16), *pieces))
    gate_grads, up_grads, down_grads = call(
        functools.partial(place_kernel, ranks=ranks),
        [f32(local, block, block)] * 3,
        "v" * ranks,
        [pltpu.VMEM((block, block), F32)],
    )(*pieces)
    return input_grad, gate_grads, up_grads, down_grads


def solution(mesh):
    flat = P("dp", None, None)
    return jax.shard_map(
        on_device,
        mesh=mesh,
        in_specs=(P("dp", None), P("dp", None), flat, flat, flat, P(), P(), P()),
        out_specs=(P("dp", "mp"), flat, flat, flat),
        check_vma=False,
    )
```
